32 devices in a mesh: groups: 2 (over x), dp: 8 (over z, y), tensor: 2 (over core).
Axes of the slice: x: 2, y: 2, z: 4, core: 2. Of those that a mesh axis runs over, the one named last changes fastest.
Arguments:
- queries: bfloat16 [4096, 4096], P(('groups', 'dp'), 'tensor'), parts along dimension 0, may hold values from -6.5 to 6.5
- fresh_keys: bfloat16 [4096, 512], P(('groups', 'dp'), 'tensor'), parts along dimension 0, may hold values from -4 to 4
- fresh_values: bfloat16 [4096, 512], P(('groups', 'dp'), 'tensor'), parts along dimension 0, may hold values from -4 to 4
- key_pool_pages: bfloat16 [160, 128, 512], P(('groups', 'dp'), None, 'tensor'), parts along dimension 0, may hold values from -4 to 4
- value_pool_pages: bfloat16 [160, 128, 512], P(('groups', 'dp'), None, 'tensor'), parts along dimension 0, may hold values from -4 to 4
- block_table: int32 [16, 8], P(('groups', 'dp')), parts along dimension 0, may hold values from 0 to 9, as said below
- prefix_lengths: int32 [16], P('groups'), parts along dimension 0, may hold values from 0 to 1024, as said below
- out_weight: bfloat16 [4096, 4096], P('tensor', 'dp'), may hold values from -0.09375 to 0.09375
Outputs:
- output: bfloat16 [4096, 4096], P(('groups', 'dp'), 'tensor'), parts along dimension 0
The draws below stay inside these ranges and needn't reach their ends.
There are 2 independent parts, one for each index of `groups`. The reference program is written for one: setup_inputs(seed, part) draws one part's arguments, and reference() takes and returns one part's arrays. A program takes and returns all parts, laid end to end along the dimension named above; an argument that names none is the same for every part. Nothing has to cross between parts.
Inputs may be any that keep to these rules, and one draw needn't show every extreme that they name: `block_table`: each row holds distinct pages of the request's own pool of 10 pages. `prefix_lengths`: some request has exactly 1024 cached tokens and some has none.
All inputs are finite; a program needn't handle non-finite values.
Results may differ from the reference program's by a relative error of at most 0.0095.
Values may be sent and summed in bfloat16 or wider, within the bound.
A program may use at most 128 MiB of HBM per device.

```python
import jax
import jax.numpy as jnp
from jax import lax

D = 4096
HEAD_SIZE = 128
KEY_VALUE_HEADS = 4
QUERY_GROUP = 8
HQ = 32
REQUEST_TOKENS = 256
PAGE_TOKENS = 128
PAGES = 8
MAX_CACHED = 1024
POOL_PAGES = 10
REQUEST_COUNT = 8
ALL_TOKENS = 2048


def draw_queries(key, part):
    window_width = HQ * HEAD_SIZE
    base_random_draw = jnp.clip(jax.random.normal(jax.random.fold_in(key, 11), (REQUEST_COUNT, REQUEST_TOKENS, window_width), jnp.float32), -4.0, 4.0)
    return base_random_draw.reshape(ALL_TOKENS, window_width).astype(jnp.bfloat16)


def draw_fresh_keys(key, part):
    window_width = KEY_VALUE_HEADS * HEAD_SIZE
    base_random_draw = jnp.clip(jax.random.normal(jax.random.fold_in(key, 13), (REQUEST_COUNT, REQUEST_TOKENS, window_width), jnp.float32), -4.0, 4.0)
    return base_random_draw.reshape(ALL_TOKENS, window_width).astype(jnp.bfloat16)


def draw_prefix_lengths(key, part):
    first_draw = jax.random.randint(jax.random.fold_in(key, 21), (REQUEST_COUNT,), 0, MAX_CACHED + 1)
    second_draw = jax.random.randint(jax.random.fold_in(key, 22), (REQUEST_COUNT,), 0, MAX_CACHED + 1)
    lengths = first_draw * second_draw // MAX_CACHED
    chosen = jax.random.randint(jax.random.fold_in(key, 23), (), 0, REQUEST_COUNT)
    lengths = lengths.at[chosen].set(MAX_CACHED)
    emptied = (chosen + 1 + jax.random.randint(jax.random.fold_in(key, 24), (), 0, REQUEST_COUNT - 1)) % REQUEST_COUNT
    return lengths.at[emptied].set(0).astype(jnp.int32)


def draw_block_table(key, part):
    subkeys = jax.random.split(jax.random.fold_in(key, 31), REQUEST_COUNT)
    return jax.vmap(lambda subkey: jax.random.permutation(subkey, POOL_PAGES)[:PAGES])(subkeys).astype(jnp.int32)


def levels(key, dims, cuts, low, high):
    gain = 1.0
    for axis_at, parts in cuts:
        heights = jax.random.uniform(jax.random.fold_in(jax.random.fold_in(key, 6), axis_at), (parts,), jnp.float32, low / len(cuts), high / len(cuts))
        gain = gain * jnp.repeat(jnp.exp(heights), dims[axis_at] // parts).reshape((-1,) + (1,) * (len(dims) - 1 - axis_at))
    return gain


def scatter_about(stream_key, dims, scale, bound, shards=(), held_as=jnp.bfloat16):
    entries = jax.random.normal(stream_key, dims, jnp.float32) * scale
    if len(shards) > 0:
        entries = levels(stream_key, dims, shards, -0.22, 0.18) * entries
    return jnp.clip(entries, min=-bound, max=bound).astype(held_as)


def setup_inputs(seed: int = 0, part: int = 0) -> dict:
    key_of = jax.random.split(jax.random.key(seed), 9)
    part_keys = jax.random.split(jax.random.fold_in(key_of[8], part), 9)
    return {
        "queries": draw_queries(jax.random.fold_in(jax.random.fold_in(key_of[8], part), 71), part),
        "fresh_keys": draw_fresh_keys(jax.random.fold_in(jax.random.fold_in(key_of[8], part), 71), part),
        "fresh_values": scatter_about(part_keys[2], (ALL_TOKENS, KEY_VALUE_HEADS * HEAD_SIZE), 1.0, 4.0, ((0, 8), (1, 2))),
        "key_pool_pages": scatter_about(part_keys[3], (REQUEST_COUNT * POOL_PAGES, PAGE_TOKENS, KEY_VALUE_HEADS * HEAD_SIZE), 1.0, 4.0, ((0, 8), (2, 2))),
        "value_pool_pages": scatter_about(part_keys[4], (REQUEST_COUNT * POOL_PAGES, PAGE_TOKENS, KEY_VALUE_HEADS * HEAD_SIZE), 1.0, 4.0, ((0, 8), (2, 2))),
        "block_table": draw_block_table(jax.random.fold_in(jax.random.fold_in(key_of[8], part), 71), part),
        "prefix_lengths": draw_prefix_lengths(jax.random.fold_in(jax.random.fold_in(key_of[8], part), 71), part),
        "out_weight": scatter_about(key_of[7], (HQ * HEAD_SIZE, D), (HQ * HEAD_SIZE) ** -0.5, 0.09375, ((0, 2), (1, 8))),
    }


def reference(queries, fresh_keys, fresh_values, key_pool_pages, value_pool_pages, block_table, prefix_lengths, out_weight):
    score_scale = HEAD_SIZE ** -0.5

    def single(request_index):
        query_block = lax.dynamic_slice_in_dim(queries, request_index * REQUEST_TOKENS, REQUEST_TOKENS, 0).astype(jnp.float32).reshape(REQUEST_TOKENS, KEY_VALUE_HEADS, QUERY_GROUP, HEAD_SIZE)
        window_keys = lax.dynamic_slice_in_dim(fresh_keys, request_index * REQUEST_TOKENS, REQUEST_TOKENS, 0).reshape(REQUEST_TOKENS, KEY_VALUE_HEADS, HEAD_SIZE)
        window_values = lax.dynamic_slice_in_dim(fresh_values, request_index * REQUEST_TOKENS, REQUEST_TOKENS, 0).reshape(REQUEST_TOKENS, KEY_VALUE_HEADS, HEAD_SIZE)
        pool_page_block = lax.dynamic_slice_in_dim(key_pool_pages, request_index * POOL_PAGES, POOL_PAGES, 0)
        value_tile_block = lax.dynamic_slice_in_dim(value_pool_pages, request_index * POOL_PAGES, POOL_PAGES, 0)
        request_pages = block_table[request_index]
        stored_keys = jnp.take(pool_page_block, request_pages, axis=0).reshape(MAX_CACHED, KEY_VALUE_HEADS, HEAD_SIZE)
        stored_values = jnp.take(value_tile_block, request_pages, axis=0).reshape(MAX_CACHED, KEY_VALUE_HEADS, HEAD_SIZE)
        all_keys = jnp.concatenate([stored_keys, window_keys], 0).astype(jnp.float32)
        all_values = jnp.concatenate([stored_values, window_values], 0).astype(jnp.float32)
        key_index = jnp.arange(MAX_CACHED + REQUEST_TOKENS, dtype=jnp.int32)
        token_index = jnp.arange(REQUEST_TOKENS, dtype=jnp.int32)
        length = prefix_lengths[request_index]
        visible = jnp.where(key_index[None, :] < MAX_CACHED, key_index[None, :] < length,
                            (key_index[None, :] - MAX_CACHED) <= token_index[:, None])
        scores = jnp.einsum('tkgd,skd->kgts', query_block, all_keys) * score_scale
        scores = jnp.where(visible[None, None], scores, jnp.float32(-1e30))
        row_peak = scores.max(-1, keepdims=True)
        weights = jnp.where(visible[None, None], jnp.exp(scores - row_peak), jnp.float32(0.0))
        weight_sum = weights.sum(-1)
        rounded = lax.optimization_barrier(weights.astype(jnp.bfloat16)).astype(jnp.float32)
        weighted = jnp.einsum('kgts,skd->kgtd', rounded, all_values)
        attended = (weighted / weight_sum[..., None]).astype(jnp.bfloat16)
        return attended.transpose(2, 0, 1, 3).reshape(REQUEST_TOKENS, HQ * HEAD_SIZE)

    per_request = lax.map(single, jnp.arange(REQUEST_COUNT, dtype=jnp.int32))
    attended = per_request.reshape(ALL_TOKENS, HQ * HEAD_SIZE)
    return jnp.dot(attended, out_weight, preferred_element_type=jnp.float32).astype(jnp.bfloat16)
```

```python
import functools

import jax
import jax.numpy as jnp
from jax import lax
from jax.experimental import pallas as pl
from jax.experimental.pallas import tpu as pltpu
from jax.sharding import PartitionSpec as P

HEAD_SIZE = 128
QUERY_GROUP = 8
PAGE_TOKENS = 128
CHUNK = 256
SCALE = HEAD_SIZE ** (-0.5) * 1.4426950408889634
MASKED = -1e30


def kernel(
    line, q_ref, fk_ref, fv_ref, kp_ref, vp_ref, table_ref, len_ref, w_ref, out_ref,
    wbuf, act, stage, keys, values, bias,
    w_recv, w_next, w_side, own_send, act_recv, act_send, act_fwd, out_send, out_recv,
):
    group, dp, core = lax.axis_index("groups"), lax.axis_index("dp"), lax.axis_index("tensor")
    z, y = dp // 2, dp % 2
    half = group % 2
    cousin = group + 1 - 2 * half
    other = 1 - core
    peer = z * 2 + 1 - y
    shards = line // 2
    part, cols = w_ref.shape
    tokens = q_ref.shape[0]
    per_core = part // CHUNK
    per_half = per_core // 2
    own_core = z // shards
    own_slot = z - own_core * shards
    wide = act.shape[2] // 2
    step_cols = wide // per_core
    heads_per_step = step_cols // HEAD_SIZE
    heads_per_kv = QUERY_GROUP
    tile = min(cols, 256)
    tiles = cols // tile

    def remote(src, dst, send, recv, where):
        return pltpu.make_async_remote_copy(
            src_ref=src, dst_ref=dst, send_sem=send, recv_sem=recv,
            device_id=where, device_id_type=pl.DeviceIdType.MESH,
        )

    def rows(k):
        return pl.ds(pl.multiple_of(k * CHUNK, CHUNK), CHUNK)

    barrier = pltpu.get_barrier_semaphore()

    def greet(where):
        pl.semaphore_signal(barrier, inc=1, device_id=where, device_id_type=pl.DeviceIdType.MESH)

    greet((group, dp, other))
    greet((cousin, dp, core))
    greet((group, peer, core))

    @pl.when(z > 0)
    def _():
        greet((group, dp - 2, core))
        greet((group, dp - 2, other))

    @pl.when(z < line - 1)
    def _():
        greet((group, dp + 2, core))
        greet((group, dp + 2, other))

    neighbours = jnp.where(z > 0, 2, 0) + jnp.where(z < line - 1, 2, 0)
    pl.semaphore_wait(barrier, 3 + neighbours)

    def own_copy(k, side):
        slab = core * per_core + k
        where = (group, dp + 2 * side, own_core) if side else (group, dp, other)
        return remote(
            w_ref.at[rows(k)], wbuf.at[own_slot, rows(slab)],
            own_send.at[side + 1, k], w_recv.at[own_slot, slab], where,
        )

    def own_local(k):
        slab = core * per_core + k
        return pltpu.make_async_copy(
            w_ref.at[rows(k)], wbuf.at[own_slot, rows(slab)], w_recv.at[own_slot, slab]
        )

    def each_own(act_on):
        def one(j, carry):
            k = half * per_half + j

            @pl.when(z > 0)
            def _():
                act_on(own_copy(k, -1))

            @pl.when(z < line - 1)
            def _():
                act_on(own_copy(k, 1))

            return carry

        lax.fori_loop(0, per_half, one, 0)

        @pl.when(core != own_core)
        def _():
            lax.fori_loop(0, per_core, lambda k, carry: (act_on(own_copy(k, 0)), carry)[1], 0)

    each_own(lambda copy: copy.start())

    @pl.when(core == own_core)
    def _():
        lax.fori_loop(0, per_core, lambda k, carry: (own_local(k).start(), carry)[1], 0)

    def slab_of(i, which):
        return (i % 2) * per_core + which * per_half + i // 2

    def landed(slot, slab):
        remote(
            wbuf.at[slot, rows(slab)], wbuf.at[slot, rows(slab)],
            w_next.at[slot, slab], w_recv.at[slot, slab], (group, dp, other),
        ).wait_recv()

    def next_copy(slot, slab, step):
        return remote(
            wbuf.at[slot, rows(slab)], wbuf.at[slot, rows(slab)],
            w_next.at[slot, slab], w_recv.at[slot, slab], (group, dp + 2 * step, core),
        )

    def side_copy(slot, slab):
        return remote(
            wbuf.at[slot, rows(slab)], wbuf.at[slot, rows(slab)],
            w_side.at[slot, slab], w_recv.at[slot, slab], (cousin, dp, core),
        )

    def pass_on(slot, origin, i):
        slab = slab_of(i, half)
        landed(slot, slab)

        @pl.when(jnp.logical_and(origin < z, z < line - 1))
        def _():
            next_copy(slot, slab, 1).start()

        @pl.when(jnp.logical_and(origin > z, z > 0))
        def _():
            next_copy(slot, slab, -1).start()

        side_copy(slot, slab).start()

    length = len_ref[dp]
    cached = table_ref.shape[1] * PAGE_TOKENS
    for j in range(table_ref.shape[1]):
        page = table_ref[0, j]
        keys[j * PAGE_TOKENS:(j + 1) * PAGE_TOKENS, :] = kp_ref[page]
        values[j * PAGE_TOKENS:(j + 1) * PAGE_TOKENS, :] = vp_ref[page]
    keys[cached:, :] = fk_ref[...]
    values[cached:, :] = fv_ref[...]
    position = lax.broadcasted_iota(jnp.int32, (tokens, cached), 1)
    bias[:, :cached] = jnp.where(position < length, 0.0, MASKED)
    bias[:, cached:] = jnp.where(
        lax.broadcasted_iota(jnp.int32, (tokens, tokens), 1)
        <= lax.broadcasted_iota(jnp.int32, (tokens, tokens), 0),
        0.0, MASKED,
    )

    def act_cols(slab):
        return pl.ds(pl.multiple_of(slab * step_cols, step_cols), step_cols)

    def act_copy(i, to_peer):
        slab = core * per_core + i
        src = act.at[0, :, act_cols(slab)]
        if to_peer:
            return remote(src, act.at[1, :, act_cols(slab)], act_send.at[1, i],
                          act_recv.at[1, slab], (group, peer, core))
        return remote(src, src, act_send.at[0, i], act_recv.at[0, slab], (group, dp, other))

    def act_forward(i):
        slab = core * per_core + i
        ref = act.at[1, :, act_cols(slab)]
        return remote(ref, ref, act_fwd.at[i], act_recv.at[1, slab], (group, dp, other))

    def act_landed(block, slab):
        ref = act.at[block, :, act_cols(slab)]
        remote(ref, ref, act_fwd.at[0], act_recv.at[block, slab], (group, dp, other)).wait_recv()

    def relay(i):
        act_landed(1, core * per_core + i)
        act_forward(i).start()

    lag = 2

    def attention_step(i, carry):
        kv = (i * heads_per_step) // heads_per_kv
        kv_cols = pl.ds(pl.multiple_of(kv * HEAD_SIZE, HEAD_SIZE), HEAD_SIZE)
        for n in range(heads_per_step):
            head = i * heads_per_step + n
            q = q_ref[:, pl.ds(pl.multiple_of(head * HEAD_SIZE, HEAD_SIZE), HEAD_SIZE)]
            scores = lax.dot_general(
                q, keys[:, kv_cols], (((1,), (1,)), ((), ())), preferred_element_type=jnp.float32
            )
            scores = scores * SCALE + bias[...]
            weights = jnp.exp2(scores - jnp.max(scores, axis=-1, keepdims=True))
            total = jnp.sum(weights, axis=-1, keepdims=True)
            weighted = jnp.dot(
                weights.astype(jnp.bfloat16), values[:, kv_cols], preferred_element_type=jnp.float32
            )
            start = core * wide + head * HEAD_SIZE
            act[0, :, pl.ds(pl.multiple_of(start, HEAD_SIZE), HEAD_SIZE)] = (
                weighted / total
            ).astype(jnp.bfloat16)
        act_copy(i, True).start()
        act_copy(i, False).start()
        for side in (-1, 1):
            origin = z + side

            @pl.when(jnp.logical_and(
                jnp.logical_and(origin >= core * shards, origin < (core + 1) * shards), True))
            def _():
                pass_on(origin - core * shards, origin, i)

        @pl.when(i >= lag)
        def _():
            relay(i - lag)

        return carry

    lax.fori_loop(0, per_core, attention_step, 0)
    for i in range(per_core - lag, per_core):
        relay(i)

    def origin_of(p):
        low = core * shards
        inside = low + (z - low + p + shards * line) % shards
        return jnp.where(z < low, low + p, jnp.where(z >= low + shards, low + shards - 1 - p, inside))

    def out_cols(origin, n):
        start = (origin * 2 + y - core * 2 * shards) * cols + n * tile
        return pl.ds(pl.multiple_of(start, 128), tile)

    def out_copy(slot, n, column):
        return remote(
            stage.at[slot, n], out_ref.at[:, column], out_send.at[slot, n],
            out_recv.at[slot, n], (group, peer, core),
        )

    def product(block, slot, n):
        return jnp.dot(
            act[block], wbuf[slot, :, pl.ds(pl.multiple_of(n * tile, 128), tile)],
            preferred_element_type=jnp.float32,
        ).astype(jnp.bfloat16)

    def piece(origin, m):
        slot = origin - core * shards
        n = m % tiles
        column = out_cols(origin, n)

        @pl.when(m < tiles)
        def _():
            stage[slot, n] = product(1, slot, n)
            out_copy(slot, n, column).start()

        @pl.when(m >= tiles)
        def _():
            out_ref[:, column] = product(0, slot, n)

    def rest_landed(origin):
        slot = origin - core * shards

        def one(i, carry):
            landed(slot, slab_of(i, 1 - half))

            @pl.when(origin == z)
            def _():
                landed(slot, slab_of(i, half))

            return carry

        lax.fori_loop(0, per_core, one, 0)

    def acts_landed():
        def one(i, carry):
            act_landed(0, other * per_core + i)
            act_landed(1, other * per_core + i)
            return carry

        lax.fori_loop(0, per_core, one, 0)

    def shard_step(p, carry):
        origin = origin_of(p)
        before = origin_of(jnp.maximum(p - 1, 0))

        def chunk_step(i, inner):
            @pl.when(jnp.logical_or(origin > z + 1, origin < z - 1))
            def _():
                pass_on(origin - core * shards, origin, i)

            @pl.when(jnp.logical_and(p > 0, i == 1))
            def _():
                @pl.when(p == 1)
                def _():
                    acts_landed()

                rest_landed(before)

            @pl.when(jnp.logical_and(jnp.logical_and(p > 0, i % 2 == 1), i // 2 < 2 * tiles))
            def _():
                piece(before, i // 2)

            return inner

        lax.fori_loop(0, per_core, chunk_step, 0)
        return carry

    lax.fori_loop(0, shards, shard_step, 0)
    if shards == 1:
        acts_landed()
    last = origin_of(shards - 1)
    rest_landed(last)
    lax.fori_loop(0, 2 * tiles, lambda m, carry: (piece(last, m), carry)[1], 0)

    def finish(slot, carry):
        origin = core * shards + slot
        for n in range(tiles):
            start = (origin * 2 + 1 - y - core * 2 * shards) * cols + n * tile
            copy = out_copy(slot, n, pl.ds(pl.multiple_of(start, 128), tile))
            copy.wait_recv()
            copy.wait_send()

        @pl.when(origin != z)
        def _():
            def one(i, inner):
                slab = slab_of(i, half)

                @pl.when(jnp.logical_and(origin < z, z < line - 1))
                def _():
                    next_copy(slot, slab, 1).wait_send()

                @pl.when(jnp.logical_and(origin > z, z > 0))
                def _():
                    next_copy(slot, slab, -1).wait_send()

                side_copy(slot, slab).wait_send()
                return inner

            lax.fori_loop(0, per_core, one, 0)

        return carry

    lax.fori_loop(0, shards, finish, 0)

    def acts_sent(i, carry):
        act_copy(i, True).wait_send()
        act_copy(i, False).wait_send()
        act_forward(i).wait_send()
        return carry

    lax.fori_loop(0, per_core, acts_sent, 0)
    each_own(lambda copy: copy.wait_send())


def shards_program(line, queries, fresh_keys, fresh_values, key_pages, value_pages, table, lengths, weight):
    tokens, wide = queries.shape
    part, cols = weight.shape
    per_core = part // CHUNK
    shards = line // 2
    tile = min(cols, 256)
    tiles = cols // tile
    span = table.shape[1] * PAGE_TOKENS + tokens
    kv_width = fresh_keys.shape[1]
    out_width = 2 * shards * cols
    vmem = pl.BlockSpec(memory_space=pltpu.VMEM)
    smem = pl.BlockSpec(memory_space=pltpu.SMEM)
    dma = pltpu.SemaphoreType.DMA
    heads = wide // HEAD_SIZE
    flops = 4 * heads * tokens * span * HEAD_SIZE + 2 * 2 * tokens * 2 * part * shards * cols
    return pl.pallas_call(
        functools.partial(kernel, line),
        out_shape=jax.ShapeDtypeStruct((tokens, out_width), jnp.bfloat16),
        in_specs=[vmem, vmem, vmem, vmem, vmem, smem, smem, pl.BlockSpec(memory_space=pl.ANY)],
        out_specs=vmem,
        scratch_shapes=[
            pltpu.VMEM((shards, 2 * part, cols), jnp.bfloat16),
            pltpu.VMEM((2, tokens, 2 * wide), jnp.bfloat16),
            pltpu.VMEM((shards, tiles, tokens, tile), jnp.bfloat16),
            pltpu.VMEM((span, kv_width), jnp.bfloat16),
            pltpu.VMEM((span, kv_width), jnp.bfloat16),
            pltpu.VMEM((tokens, span), jnp.float32),
            dma((shards, 2 * per_core)),
            dma((shards, 2 * per_core)),
            dma((shards, 2 * per_core)),
            dma((3, per_core)),
            dma((2, 2 * per_core)),
            dma((2, per_core)),
            dma((per_core,)),
            dma((shards, tiles)),
            dma((shards, tiles)),
        ],
        compiler_params=pltpu.CompilerParams(
            collective_id=0, has_side_effects=True, vmem_limit_bytes=60 * 1024 * 1024
        ),
        cost_estimate=pl.CostEstimate(
            flops=flops, bytes_accessed=8 * 1024 * 1024, transcendentals=heads * tokens * span
        ),
    )(queries, fresh_keys, fresh_values, key_pages, value_pages, table, lengths, weight)


def solution(mesh):
    return jax.shard_map(
        functools.partial(shards_program, mesh.shape["dp"] // 2),
        mesh=mesh,
        in_specs=(
            P(("groups", "dp"), "tensor"),
            P(("groups", "dp"), "tensor"),
            P(("groups", "dp"), "tensor"),
            P(("groups", "dp"), None, "tensor"),
            P(("groups", "dp"), None, "tensor"),
            P(("groups", "dp"), None),
            P("groups"),
            P("tensor", "dp"),
        ),
        out_specs=P(("groups", "dp"), "tensor"),
        check_vma=False,
    )
```

```python
import functools

import jax
import jax.numpy as jnp
from jax import lax
from jax.experimental import pallas as pl
from jax.experimental.pallas import tpu as pltpu
from jax.sharding import PartitionSpec as P

HEAD_SIZE = 128
QUERY_GROUP = 8
PAGE_TOKENS = 128
CHUNK = 256
SCALE = HEAD_SIZE ** (-0.5) * 1.4426950408889634
MASKED = -1e30


def kernel(
    line, q_ref, fk_ref, fv_ref, kp_ref, vp_ref, table_ref, len_ref, w_ref, out_ref,
    wbuf, act, stage, keys, values, bias,
    w_recv, w_next, w_x, w_y, own_send, act_recv, act_send, act_fwd, out_send, out_recv,
):
    group, dp, core = lax.axis_index("groups"), lax.axis_index("dp"), lax.axis_index("tensor")
    z, y = dp // 2, dp % 2
    half, parity = group % 2, z % 2
    cousin = group + 1 - 2 * half
    other = 1 - core
    beside = z * 2 + 1 - y
    peer = (z + 1 - 2 * parity) * 2 + y
    span = line // 2
    planes = span // 2
    part, cols = w_ref.shape
    tokens = q_ref.shape[0]
    per_core = part // CHUNK
    per_half = per_core // 2
    own_core = z // span
    wide = act.shape[2] // 2
    step_cols = wide // per_core
    heads_per_step = step_cols // HEAD_SIZE
    heads_per_kv = QUERY_GROUP
    tile = min(cols, 256)
    tiles = cols // tile
    over_y = per_core * 5 // 8

    def remote(src, dst, send, recv, where):
        return pltpu.make_async_remote_copy(
            src_ref=src, dst_ref=dst, send_sem=send, recv_sem=recv,
            device_id=where, device_id_type=pl.DeviceIdType.MESH,
        )

    def rows(k):
        return pl.ds(pl.multiple_of(k * CHUNK, CHUNK), CHUNK)

    def slot_of(origin, side):
        return (origin % span // 2) * 2 + side

    barrier = pltpu.get_barrier_semaphore()

    def greet(where):
        pl.semaphore_signal(barrier, inc=1, device_id=where, device_id_type=pl.DeviceIdType.MESH)

    greet((group, dp, other))
    greet((cousin, dp, core))
    greet((group, peer, core))
    greet((group, beside, core))
    greet((group, beside, other))

    @pl.when(z > 1)
    def _():
        greet((group, dp - 4, core))
        greet((group, dp - 4, other))

    @pl.when(z < line - 2)
    def _():
        greet((group, dp + 4, core))
        greet((group, dp + 4, other))

    neighbours = jnp.where(z > 1, 2, 0) + jnp.where(z < line - 2, 2, 0)
    pl.semaphore_wait(barrier, 5 + neighbours)

    def own_copy(k, way):
        slab = core * per_core + k
        where = (
            (group, dp - 4, own_core), (group, dp + 4, own_core),
            (group, beside, own_core), (group, dp, other),
        )[way]
        slot = slot_of(z, y)
        return remote(
            w_ref.at[rows(k)], wbuf.at[slot, rows(slab)],
            own_send.at[way, k], w_recv.at[slot, slab], where,
        )

    def own_local(k):
        slab = core * per_core + k
        slot = slot_of(z, y)
        return pltpu.make_async_copy(
            w_ref.at[rows(k)], wbuf.at[slot, rows(slab)], w_recv.at[slot, slab]
        )

    def each_own(act_on):
        def one(j, carry):
            k = half * per_half + j
            act_on(own_copy(k, 2))

            @pl.when(z > 1)
            def _():
                act_on(own_copy(k, 0))

            @pl.when(z < line - 2)
            def _():
                act_on(own_copy(k, 1))

            return carry

        lax.fori_loop(0, per_half, one, 0)

        @pl.when(core != own_core)
        def _():
            lax.fori_loop(0, per_core, lambda k, carry: (act_on(own_copy(k, 3)), carry)[1], 0)

    each_own(lambda copy: copy.start())

    @pl.when(core == own_core)
    def _():
        lax.fori_loop(0, per_core, lambda k, carry: (own_local(k).start(), carry)[1], 0)

    def slab_of(i, which):
        return (i % 2) * per_core + which * per_half + i // 2

    def forward(sems, slot, slab, where):
        ref = wbuf.at[slot, rows(slab)]
        return remote(ref, ref, sems.at[slot, slab], w_recv.at[slot, slab], where)

    def landed(slot, slab):
        forward(w_x, slot, slab, (cousin, dp, core)).wait_recv()

    def to_x(slot, slab):
        return forward(w_x, slot, slab, (cousin, dp, core))

    def to_y(slot, slab):
        return forward(w_y, slot, slab, (group, beside, core))

    def z_sends(origin, i, act_on):
        slot, slab = slot_of(origin, y), slab_of(i, half)

        @pl.when(jnp.logical_and(origin < z, z < line - 2))
        def _():
            act_on(forward(w_next, slot, slab, (group, dp + 4, core)))

        @pl.when(jnp.logical_and(origin > z, z > 1))
        def _():
            act_on(forward(w_next, slot, slab, (group, dp - 4, core)))

        act_on(to_x(slot, slab))
        act_on(to_y(slot, slab))

    def x_sends(origin, i, act_on):
        @pl.when(i < over_y)
        def _():
            act_on(to_y(slot_of(origin, y), slab_of(i, 1 - half)))

    def y_sends(origin, i, act_on):
        @pl.when(jnp.logical_or(origin == z, i >= over_y))
        def _():
            act_on(to_x(slot_of(origin, 1 - y), slab_of(i, half)))

    def start(copy):
        copy.start()

    def z_step(origin, i):
        landed(slot_of(origin, y), slab_of(i, half))
        z_sends(origin, i, start)

    def xy_step(origin, i):
        landed(slot_of(origin, y), slab_of(i, 1 - half))
        x_sends(origin, i, start)
        y_step(origin, i)

    def y_step(origin, i):
        landed(slot_of(origin, 1 - y), slab_of(i, half))
        y_sends(origin, i, start)

    def origin_of(p):
        low = core * span
        inside = low + (z - low + 2 * p + span * line) % span
        near = low + parity + 2 * p
        far = low + span - 2 + parity - 2 * p
        return jnp.where(z < low, near, jnp.where(z >= low + span, far, inside))

    first = origin_of(0)

    length = len_ref[dp]
    cached = table_ref.shape[1] * PAGE_TOKENS
    for j in range(table_ref.shape[1]):
        page = table_ref[0, j]
        keys[j * PAGE_TOKENS:(j + 1) * PAGE_TOKENS, :] = kp_ref[page]
        values[j * PAGE_TOKENS:(j + 1) * PAGE_TOKENS, :] = vp_ref[page]
    keys[cached:, :] = fk_ref[...]
    values[cached:, :] = fv_ref[...]
    position = lax.broadcasted_iota(jnp.int32, (tokens, cached), 1)
    bias[:, :cached] = jnp.where(position < length, 0.0, MASKED)
    bias[:, cached:] = jnp.where(
        lax.broadcasted_iota(jnp.int32, (tokens, tokens), 1)
        <= lax.broadcasted_iota(jnp.int32, (tokens, tokens), 0),
        0.0, MASKED,
    )

    def act_cols(slab):
        return pl.ds(pl.multiple_of(slab * step_cols, step_cols), step_cols)

    def act_copy(i, to_peer):
        slab = core * per_core + i
        src = act.at[0, :, act_cols(slab)]
        if to_peer:
            return remote(src, act.at[1, :, act_cols(slab)], act_send.at[1, i],
                          act_recv.at[1, slab], (group, peer, core))
        return remote(src, src, act_send.at[0, i], act_recv.at[0, slab], (group, dp, other))

    def act_forward(i):
        slab = core * per_core + i
        ref = act.at[1, :, act_cols(slab)]
        return remote(ref, ref, act_fwd.at[i], act_recv.at[1, slab], (group, dp, other))

    def act_landed(block, slab):
        ref = act.at[block, :, act_cols(slab)]
        remote(ref, ref, act_fwd.at[0], act_recv.at[block, slab], (group, dp, other)).wait_recv()

    def relay(i):
        act_landed(1, core * per_core + i)
        act_forward(i).start()

    lag = 2

    def attention_step(i, carry):
        kv = (i * heads_per_step) // heads_per_kv
        kv_cols = pl.ds(pl.multiple_of(kv * HEAD_SIZE, HEAD_SIZE), HEAD_SIZE)
        for n in range(heads_per_step):
            head = i * heads_per_step + n
            q = q_ref[:, pl.ds(pl.multiple_of(head * HEAD_SIZE, HEAD_SIZE), HEAD_SIZE)]
            scores = lax.dot_general(
                q, keys[:, kv_cols], (((1,), (1,)), ((), ())), preferred_element_type=jnp.float32
            )
            scores = scores * SCALE + bias[...]
            weights = jnp.exp2(scores - jnp.max(scores, axis=-1, keepdims=True))
            total = jnp.sum(weights, axis=-1, keepdims=True)
            weighted = jnp.dot(
                weights.astype(jnp.bfloat16), values[:, kv_cols], preferred_element_type=jnp.float32
            )
            start = core * wide + head * HEAD_SIZE
            act[0, :, pl.ds(pl.multiple_of(start, HEAD_SIZE), HEAD_SIZE)] = (
                weighted / total
            ).astype(jnp.bfloat16)
        act_copy(i, True).start()
        act_copy(i, False).start()
        @pl.when(core == own_core)
        def _():
            y_step(z, i)

        @pl.when(jnp.logical_and(core != own_core, i % 2 == 1))
        def _():
            z_step(first, i // 2)

        @pl.when(jnp.logical_and(core != own_core, jnp.logical_and(i % 2 == 0, i > 0)))
        def _():
            xy_step(first, i // 2 - 1)

        @pl.when(i >= lag)
        def _():
            relay(i - lag)

        return carry

    lax.fori_loop(0, per_core, attention_step, 0)
    for i in range(per_core - lag, per_core):
        relay(i)

    def out_cols(origin, side, n):
        start_col = (origin % span * 2 + side) * cols + n * tile
        return pl.ds(pl.multiple_of(start_col, 128), tile)

    def out_copy(slot, n, column):
        return remote(
            stage.at[slot, n], out_ref.at[:, column], out_send.at[slot, n],
            out_recv.at[slot, n], (group, peer, core),
        )

    def product(block, slot, n):
        return jnp.dot(
            act[block], wbuf[slot, :, pl.ds(pl.multiple_of(n * tile, 128), tile)],
            preferred_element_type=jnp.float32,
        ).astype(jnp.bfloat16)

    def project(origin, side):
        slot = slot_of(origin, side)

        def piece(m, carry):
            n = m % tiles
            column = out_cols(origin, side, n)

            @pl.when(m < tiles)
            def _():
                stage[slot, n] = product(1, slot, n)
                out_copy(slot, n, column).start()

            @pl.when(m >= tiles)
            def _():
                out_ref[:, column] = product(0, slot, n)

            return carry

        lax.fori_loop(0, 2 * tiles, piece, 0)

    def acts_landed():
        def one(i, carry):
            act_landed(0, other * per_core + i)
            act_landed(1, other * per_core + i)
            return carry

        lax.fori_loop(0, per_core, one, 0)

    def plane_step(p, carry):
        origin = origin_of(p)

        def chunk_step(m, inner):
            @pl.when(m < per_core)
            def _():
                z_step(origin, m)

            @pl.when(m > 0)
            def _():
                xy_step(origin, m - 1)

            return inner

        @pl.when(origin != z)
        def _():
            begin = jnp.where(p == 0, per_half, 0)
            lax.fori_loop(begin, per_core + 1, chunk_step, 0)

        @pl.when(p == 0)
        def _():
            acts_landed()

        def one_own(i, inner):
            landed(slot_of(origin, y), slab_of(i, 0))
            landed(slot_of(origin, y), slab_of(i, 1))
            return inner

        @pl.when(origin == z)
        def _():
            lax.fori_loop(0, per_core, one_own, 0)

        project(origin, y)

        def one(i, inner):
            landed(slot_of(origin, 1 - y), slab_of(i, 1 - half))
            return inner

        lax.fori_loop(0, per_core, one, 0)
        project(origin, 1 - y)
        return carry

    lax.fori_loop(0, planes, plane_step, 0)

    def finish(index, carry):
        origin = core * span + index * 2 + parity
        for side in (0, 1):
            for n in range(tiles):
                slot = index * 2 + side
                copy = out_copy(slot, n, out_cols(origin + 1 - 2 * parity, side, n))
                copy.wait_recv()
                copy.wait_send()

        def one(i, inner):
            @pl.when(origin != z)
            def _():
                z_sends(origin, i, lambda copy: copy.wait_send())
                x_sends(origin, i, lambda copy: copy.wait_send())

            y_sends(origin, i, lambda copy: copy.wait_send())
            return inner

        lax.fori_loop(0, per_core, one, 0)
        return carry

    lax.fori_loop(0, planes, finish, 0)

    def acts_sent(i, carry):
        act_copy(i, True).wait_send()
        act_copy(i, False).wait_send()
        act_forward(i).wait_send()
        return carry

    lax.fori_loop(0, per_core, acts_sent, 0)
    each_own(lambda copy: copy.wait_send())


def shards_program(line, queries, fresh_keys, fresh_values, key_pages, value_pages, table, lengths, weight):
    tokens, wide = queries.shape
    part, cols = weight.shape
    per_core = part // CHUNK
    shards = line // 2
    tile = min(cols, 256)
    tiles = cols // tile
    span = table.shape[1] * PAGE_TOKENS + tokens
    kv_width = fresh_keys.shape[1]
    out_width = 2 * shards * cols
    vmem = pl.BlockSpec(memory_space=pltpu.VMEM)
    smem = pl.BlockSpec(memory_space=pltpu.SMEM)
    dma = pltpu.SemaphoreType.DMA
    heads = wide // HEAD_SIZE
    flops = 4 * heads * tokens * span * HEAD_SIZE + 2 * 2 * tokens * 2 * part * shards * cols
    return pl.pallas_call(
        functools.partial(kernel, line),
        out_shape=jax.ShapeDtypeStruct((tokens, out_width), jnp.bfloat16),
        in_specs=[vmem, vmem, vmem, vmem, vmem, smem, smem, pl.BlockSpec(memory_space=pl.ANY)],
        out_specs=vmem,
        scratch_shapes=[
            pltpu.VMEM((shards, 2 * part, cols), jnp.bfloat16),
            pltpu.VMEM((2, tokens, 2 * wide), jnp.bfloat16),
            pltpu.VMEM((shards, tiles, tokens, tile), jnp.bfloat16),
            pltpu.VMEM((span, kv_width), jnp.bfloat16),
            pltpu.VMEM((span, kv_width), jnp.bfloat16),
            pltpu.VMEM((tokens, span), jnp.float32),
            dma((shards, 2 * per_core)),
            dma((shards, 2 * per_core)),
            dma((shards, 2 * per_core)),
            dma((shards, 2 * per_core)),
            dma((4, per_core)),
            dma((2, 2 * per_core)),
            dma((2, per_core)),
            dma((per_core,)),
            dma((shards, tiles)),
            dma((shards, tiles)),
        ],
        compiler_params=pltpu.CompilerParams(
            collective_id=0, has_side_effects=True, vmem_limit_bytes=60 * 1024 * 1024
        ),
        cost_estimate=pl.CostEstimate(
            flops=flops, bytes_accessed=8 * 1024 * 1024, transcendentals=heads * tokens * span
        ),
    )(queries, fresh_keys, fresh_values, key_pages, value_pages, table, lengths, weight)


def solution(mesh):
    return jax.shard_map(
        functools.partial(shards_program, mesh.shape["dp"] // 2),
        mesh=mesh,
        in_specs=(
            P(("groups", "dp"), "tensor"),
            P(("groups", "dp"), "tensor"),
            P(("groups", "dp"), "tensor"),
            P(("groups", "dp"), None, "tensor"),
            P(("groups", "dp"), None, "tensor"),
            P(("groups", "dp"), None),
            P("groups"),
            P("tensor", "dp"),
        ),
        out_specs=P(("groups", "dp"), "tensor"),
        check_vma=False,
    )
```

```python
import functools

import jax
import jax.numpy as jnp
from jax import lax
from jax.experimental import pallas as pl
from jax.experimental.pallas import tpu as pltpu
from jax.sharding import PartitionSpec as P

HEAD_SIZE = 128
QUERY_GROUP = 8
PAGE_TOKENS = 128
CHUNK = 256
SCALE = HEAD_SIZE ** (-0.5) * 1.4426950408889634
MASKED = -1e30


def kernel(
    line, q_ref, fk_ref, fv_ref, kp_ref, vp_ref, table_ref, len_ref, w_ref, out_ref,
    wbuf, act, stage, keys, values, bias,
    w_recv, w_next, w_side, own_send, act_recv, act_send, act_fwd, out_send, out_recv,
):
    group, dp, core = lax.axis_index("groups"), lax.axis_index("dp"), lax.axis_index("tensor")
    z, y = dp // 2, dp % 2
    half = group % 2
    cousin = group + 1 - 2 * half
    other = 1 - core
    peer = z * 2 + 1 - y
    shards = line // 2
    part, cols = w_ref.shape
    tokens = q_ref.shape[0]
    per_core = part // CHUNK
    per_half = per_core // 2
    own_core = z // shards
    own_slot = z - own_core * shards
    wide = act.shape[2] // 2
    step_cols = wide // per_core
    heads_per_step = step_cols // HEAD_SIZE
    heads_per_kv = QUERY_GROUP
    tile = min(cols, 256)
    tiles = cols // tile

    def remote(src, dst, send, recv, where):
        return pltpu.make_async_remote_copy(
            src_ref=src, dst_ref=dst, send_sem=send, recv_sem=recv,
            device_id=where, device_id_type=pl.DeviceIdType.MESH,
        )

    def rows(k):
        return pl.ds(pl.multiple_of(k * CHUNK, CHUNK), CHUNK)

    barrier = pltpu.get_barrier_semaphore()

    def greet(where):
        pl.semaphore_signal(barrier, inc=1, device_id=where, device_id_type=pl.DeviceIdType.MESH)

    greet((group, dp, other))
    greet((cousin, dp, core))
    greet((group, peer, core))

    @pl.when(z > 0)
    def _():
        greet((group, dp - 2, core))
        greet((group, dp - 2, other))

    @pl.when(z < line - 1)
    def _():
        greet((group, dp + 2, core))
        greet((group, dp + 2, other))

    neighbours = jnp.where(z > 0, 2, 0) + jnp.where(z < line - 1, 2, 0)
    pl.semaphore_wait(barrier, 3 + neighbours)

    def own_copy(k, side):
        slab = core * per_core + k
        where = (group, dp + 2 * side, own_core) if side else (group, dp, other)
        return remote(
            w_ref.at[rows(k)], wbuf.at[own_slot, rows(slab)],
            own_send.at[side + 1, k], w_recv.at[own_slot, slab], where,
        )

    def own_local(k):
        slab = core * per_core + k
        return pltpu.make_async_copy(
            w_ref.at[rows(k)], wbuf.at[own_slot, rows(slab)], w_recv.at[own_slot, slab]
        )

    def each_own(act_on):
        def one(j, carry):
            k = half * per_half + j

            @pl.when(z > 0)
            def _():
                act_on(own_copy(k, -1))

            @pl.when(z < line - 1)
            def _():
                act_on(own_copy(k, 1))

            return carry

        lax.fori_loop(0, per_half, one, 0)

        @pl.when(core != own_core)
        def _():
            lax.fori_loop(0, per_core, lambda k, carry: (act_on(own_copy(k, 0)), carry)[1], 0)

    each_own(lambda copy: copy.start())

    @pl.when(core == own_core)
    def _():
        lax.fori_loop(0, per_core, lambda k, carry: (own_local(k).start(), carry)[1], 0)

    def slab_of(i, which):
        return (i % 2) * per_core + which * per_half + i // 2

    def landed(slot, slab):
        remote(
            wbuf.at[slot, rows(slab)], wbuf.at[slot, rows(slab)],
            w_next.at[slot, slab], w_recv.at[slot, slab], (group, dp, other),
        ).wait_recv()

    def next_copy(slot, slab, step):
        return remote(
            wbuf.at[slot, rows(slab)], wbuf.at[slot, rows(slab)],
            w_next.at[slot, slab], w_recv.at[slot, slab], (group, dp + 2 * step, core),
        )

    def side_copy(slot, slab):
        return remote(
            wbuf.at[slot, rows(slab)], wbuf.at[slot, rows(slab)],
            w_side.at[slot, slab], w_recv.at[slot, slab], (cousin, dp, core),
        )

    def pass_on(slot, origin, i):
        slab = slab_of(i, half)
        landed(slot, slab)

        @pl.when(jnp.logical_and(origin < z, z < line - 1))
        def _():
            next_copy(slot, slab, 1).start()

        @pl.when(jnp.logical_and(origin > z, z > 0))
        def _():
            next_copy(slot, slab, -1).start()

        side_copy(slot, slab).start()

    length = len_ref[dp]
    cached = table_ref.shape[1] * PAGE_TOKENS
    for j in range(table_ref.shape[1]):
        page = table_ref[0, j]
        keys[j * PAGE_TOKENS:(j + 1) * PAGE_TOKENS, :] = kp_ref[page]
        values[j * PAGE_TOKENS:(j + 1) * PAGE_TOKENS, :] = vp_ref[page]
    keys[cached:, :] = fk_ref[...]
    values[cached:, :] = fv_ref[...]
    position = lax.broadcasted_iota(jnp.int32, (tokens, cached), 1)
    bias[:, :cached] = jnp.where(position < length, 0.0, MASKED)
    bias[:, cached:] = jnp.where(
        lax.broadcasted_iota(jnp.int32, (tokens, tokens), 1)
        <= lax.broadcasted_iota(jnp.int32, (tokens, tokens), 0),
        0.0, MASKED,
    )

    def act_cols(slab):
        return pl.ds(pl.multiple_of(slab * step_cols, step_cols), step_cols)

    def act_copy(i, to_peer):
        slab = core * per_core + i
        src = act.at[0, :, act_cols(slab)]
        if to_peer:
            return remote(src, act.at[1, :, act_cols(slab)], act_send.at[1, i],
                          act_recv.at[1, slab], (group, peer, core))
        return remote(src, src, act_send.at[0, i], act_recv.at[0, slab], (group, dp, other))

    def act_forward(i):
        slab = core * per_core + i
        ref = act.at[1, :, act_cols(slab)]
        return remote(ref, ref, act_fwd.at[i], act_recv.at[1, slab], (group, dp, other))

    def act_landed(block, slab):
        ref = act.at[block, :, act_cols(slab)]
        remote(ref, ref, act_fwd.at[0], act_recv.at[block, slab], (group, dp, other)).wait_recv()

    def relay(i):
        act_landed(1, core * per_core + i)
        act_forward(i).start()

    lag = 2

    def attention_step(i, carry):
        kv = (i * heads_per_step) // heads_per_kv
        kv_cols = pl.ds(pl.multiple_of(kv * HEAD_SIZE, HEAD_SIZE), HEAD_SIZE)
        for n in range(heads_per_step):
            head = i * heads_per_step + n
            q = q_ref[:, pl.ds(pl.multiple_of(head * HEAD_SIZE, HEAD_SIZE), HEAD_SIZE)]
            scores = lax.dot_general(
                q, keys[:, kv_cols], (((1,), (1,)), ((), ())), preferred_element_type=jnp.float32
            )
            scores = scores * SCALE + bias[...]
            weights = jnp.exp2(scores - jnp.max(scores, axis=-1, keepdims=True))
            total = jnp.sum(weights, axis=-1, keepdims=True)
            weighted = jnp.dot(
                weights.astype(jnp.bfloat16), values[:, kv_cols], preferred_element_type=jnp.float32
            )
            start = core * wide + head * HEAD_SIZE
            act[0, :, pl.ds(pl.multiple_of(start, HEAD_SIZE), HEAD_SIZE)] = (
                weighted / total
            ).astype(jnp.bfloat16)
        act_copy(i, True).start()
        act_copy(i, False).start()
        for side in (-1, 1):
            origin = z + side

            @pl.when(jnp.logical_and(
                jnp.logical_and(origin >= core * shards, origin < (core + 1) * shards), True))
            def _():
                pass_on(origin - core * shards, origin, i)

        @pl.when(i >= lag)
        def _():
            relay(i - lag)

        return carry

    lax.fori_loop(0, per_core, attention_step, 0)
    for i in range(per_core - lag, per_core):
        relay(i)

    def origin_of(p):
        low = core * shards
        inside = low + (z - low + p + shards * line) % shards
        return jnp.where(z < low, low + p, jnp.where(z >= low + shards, low + shards - 1 - p, inside))

    def out_cols(origin, n):
        start = (origin * 2 + y - core * 2 * shards) * cols + n * tile
        return pl.ds(pl.multiple_of(start, 128), tile)

    def out_copy(slot, n, column):
        return remote(
            stage.at[slot, n], out_ref.at[:, column], out_send.at[slot, n],
            out_recv.at[slot, n], (group, peer, core),
        )

    def product(block, slot, n):
        return jnp.dot(
            act[block], wbuf[slot, :, pl.ds(pl.multiple_of(n * tile, 128), tile)],
            preferred_element_type=jnp.float32,
        ).astype(jnp.bfloat16)

    def piece(origin, m):
        slot = origin - core * shards
        n = m % tiles
        column = out_cols(origin, n)

        @pl.when(m < tiles)
        def _():
            stage[slot, n] = product(1, slot, n)
            out_copy(slot, n, column).start()

        @pl.when(m >= tiles)
        def _():
            out_ref[:, column] = product(0, slot, n)

    def rest_landed(origin):
        slot = origin - core * shards

        def one(i, carry):
            landed(slot, slab_of(i, 1 - half))

            @pl.when(origin == z)
            def _():
                landed(slot, slab_of(i, half))

            return carry

        lax.fori_loop(0, per_core, one, 0)

    def acts_landed():
        def one(i, carry):
            act_landed(0, other * per_core + i)
            act_landed(1, other * per_core + i)
            return carry

        lax.fori_loop(0, per_core, one, 0)

    def shard_step(p, carry):
        origin = origin_of(p)
        before = origin_of(jnp.maximum(p - 1, 0))

        def chunk_step(i, inner):
            @pl.when(jnp.logical_or(origin > z + 1, origin < z - 1))
            def _():
                pass_on(origin - core * shards, origin, i)

            return inner

        lax.fori_loop(0, per_core, chunk_step, 0)

        @pl.when(p > 0)
        def _():
            @pl.when(p == 1)
            def _():
                acts_landed()

            rest_landed(before)
            lax.fori_loop(0, 2 * tiles, lambda m, inner: (piece(before, m), inner)[1], 0)

        return carry

    lax.fori_loop(0, shards, shard_step, 0)
    if shards == 1:
        acts_landed()
    last = origin_of(shards - 1)
    rest_landed(last)
    lax.fori_loop(0, 2 * tiles, lambda m, carry: (piece(last, m), carry)[1], 0)

    def finish(slot, carry):
        origin = core * shards + slot
        for n in range(tiles):
            start = (origin * 2 + 1 - y - core * 2 * shards) * cols + n * tile
            copy = out_copy(slot, n, pl.ds(pl.multiple_of(start, 128), tile))
            copy.wait_recv()
            copy.wait_send()

        @pl.when(origin != z)
        def _():
            def one(i, inner):
                slab = slab_of(i, half)

                @pl.when(jnp.logical_and(origin < z, z < line - 1))
                def _():
                    next_copy(slot, slab, 1).wait_send()

                @pl.when(jnp.logical_and(origin > z, z > 0))
                def _():
                    next_copy(slot, slab, -1).wait_send()

                side_copy(slot, slab).wait_send()
                return inner

            lax.fori_loop(0, per_core, one, 0)

        return carry

    lax.fori_loop(0, shards, finish, 0)

    def acts_sent(i, carry):
        act_copy(i, True).wait_send()
        act_copy(i, False).wait_send()
        act_forward(i).wait_send()
        return carry

    lax.fori_loop(0, per_core, acts_sent, 0)
    each_own(lambda copy: copy.wait_send())


def shards_program(line, queries, fresh_keys, fresh_values, key_pages, value_pages, table, lengths, weight):
    tokens, wide = queries.shape
    part, cols = weight.shape
    per_core = part // CHUNK
    shards = line // 2
    tile = min(cols, 256)
    tiles = cols // tile
    span = table.shape[1] * PAGE_TOKENS + tokens
    kv_width = fresh_keys.shape[1]
    out_width = 2 * shards * cols
    vmem = pl.BlockSpec(memory_space=pltpu.VMEM)
    smem = pl.BlockSpec(memory_space=pltpu.SMEM)
    dma = pltpu.SemaphoreType.DMA
    heads = wide // HEAD_SIZE
    flops = 4 * heads * tokens * span * HEAD_SIZE + 2 * 2 * tokens * 2 * part * shards * cols
    return pl.pallas_call(
        functools.partial(kernel, line),
        out_shape=jax.ShapeDtypeStruct((tokens, out_width), jnp.bfloat16),
        in_specs=[vmem, vmem, vmem, vmem, vmem, smem, smem, pl.BlockSpec(memory_space=pl.ANY)],
        out_specs=vmem,
        scratch_shapes=[
            pltpu.VMEM((shards, 2 * part, cols), jnp.bfloat16),
            pltpu.VMEM((2, tokens, 2 * wide), jnp.bfloat16),
            pltpu.VMEM((shards, tiles, tokens, tile), jnp.bfloat16),
            pltpu.VMEM((span, kv_width), jnp.bfloat16),
            pltpu.VMEM((span, kv_width), jnp.bfloat16),
            pltpu.VMEM((tokens, span), jnp.float32),
            dma((shards, 2 * per_core)),
            dma((shards, 2 * per_core)),
            dma((shards, 2 * per_core)),
            dma((3, per_core)),
            dma((2, 2 * per_core)),
            dma((2, per_core)),
            dma((per_core,)),
            dma((shards, tiles)),
            dma((shards, tiles)),
        ],
        compiler_params=pltpu.CompilerParams(
            collective_id=0, has_side_effects=True, vmem_limit_bytes=60 * 1024 * 1024
        ),
        cost_estimate=pl.CostEstimate(
            flops=flops, bytes_accessed=8 * 1024 * 1024, transcendentals=heads * tokens * span
        ),
    )(queries, fresh_keys, fresh_values, key_pages, value_pages, table, lengths, weight)


def solution(mesh):
    return jax.shard_map(
        functools.partial(shards_program, mesh.shape["dp"] // 2),
        mesh=mesh,
        in_specs=(
            P(("groups", "dp"), "tensor"),
            P(("groups", "dp"), "tensor"),
            P(("groups", "dp"), "tensor"),
            P(("groups", "dp"), None, "tensor"),
            P(("groups", "dp"), None, "tensor"),
            P(("groups", "dp"), None),
            P("groups"),
            P("tensor", "dp"),
        ),
        out_specs=P(("groups", "dp"), "tensor"),
        check_vma=False,
    )
```
